32 devices in a mesh: region: 8 (over z, core), member: 4 (over y, x).
Axes of the slice: x: 2, y: 2, z: 4, core: 2. Of those that a mesh axis runs over, the one named last changes fastest.
Arguments:
- positions: float32 [3, 12288], P(None, ('region', 'member'))
- forces: float32 [3, 12288], P(None, ('region', 'member')), may hold values from -6 to 6
- blob_platelet: int32 [12288], P(('region', 'member')), may hold values from 0 to 8, as said below
- blob_rank: int32 [12288], P(('region', 'member')), may hold values from 0 to 161, as said below
- platelet_owner: int32 [64], P('region'), may hold values from 0 to 7, as said below
- pair_list: int32 [96, 8], P(('region', 'member')), may hold values from 0 to 23, as said below
- pair_count: int32 [96], P(('region', 'member')), may hold values from 1 to 8, as said below
- preconditioner: bfloat16 [64, 486, 486], P(('region', 'member')), may hold values from -0.25 to 0.25
Outputs:
- blob_velocity: float32 [3, 12288], P(None, ('region', 'member'))
- body_velocity: float32 [64, 486], P(('region', 'member'))
The draws below stay inside these ranges and needn't reach their ends.
Inputs may be any that keep to these rules, and one draw needn't show every extreme that they name: `blob_platelet`: in each slab every platelet id below 8 appears on exactly 162 slots, and 8 marks an empty slot. Every device holds exactly 324 live blobs, of which at most 121 belong to platelets whose owner slots lie on one member; that bound is met in every slab. `blob_rank`: the 162 blobs of one platelet have distinct ranks; empty slots have rank 0. `platelet_owner`: the 8 entries of one slab are a permutation; owner slot o lies on member o // 2 of that slab. `pair_list`: the entries of one target tile are distinct, and entry 0 is the tile itself, 6 plus its index within its slab. `pair_count`: some tile has 8 in every draw.
All inputs are finite; a program needn't handle non-finite values.
Results may differ from the reference program's by a relative error of at most 0.0029.
Values sent between devices are 32-bit elements; how exact they have to be, the bound alone decides.
A program may use at most 64 MiB of HBM per device.

```python
import math
import jax
import jax.numpy as jnp
from jax import lax

TILE = 128
PB = 162
BODY = 486
PLAT_DEV = 2
PAIRS = 8
BLOB_DEV = 384
REG_BLK = 12
REG_BLOBS = 1536
EXT_BLK = 24
PLAT_REG = 8
NPLATS = 64
NBLOCKS = 96
NBLOBS = 12288
CAP = 121
N_REGION = 8
N_MEMBER = 4


slab_width = 2.0


span_width = 4.0


def region_layout(region_key):
    order_key, share_key, latin_key, shuffle_key = jax.random.split(region_key, 4)
    owner_map = jax.random.permutation(order_key, PLAT_REG).astype(jnp.int32)
    inverse_map = jnp.zeros((PLAT_REG,), jnp.int32).at[owner_map].set(jnp.arange(PLAT_REG, dtype=jnp.int32))
    total_live = PLAT_DEV * PB
    base_share = total_live // N_MEMBER
    leftover = total_live % N_MEMBER
    swings = jax.random.randint(share_key, (N_MEMBER // 2,), 0, base_share // 2 + 1).astype(jnp.int32)
    swings = swings.at[0].set(base_share // 2)
    paired = jnp.stack([swings, -swings], axis=1).reshape(N_MEMBER)
    shares = base_share + paired + (jnp.arange(N_MEMBER) < leftover).astype(jnp.int32)
    latin_shift = jax.random.permutation(latin_key, N_MEMBER).astype(jnp.int32)
    source_ids = jnp.arange(N_MEMBER, dtype=jnp.int32)
    grid_counts = shares[(source_ids[:, None] + latin_shift[None, :]) % N_MEMBER]
    grid_starts = jnp.cumsum(grid_counts, axis=0) - grid_counts
    offsets = jnp.arange(CAP, dtype=jnp.int32)
    is_valid = offsets[None, None, :] < grid_counts[:, :, None]
    within = grid_starts[:, :, None] + offsets[None, None, :]
    owner_member = jnp.broadcast_to(source_ids[None, :, None], is_valid.shape)
    width_all = N_MEMBER * CAP
    pad_valid = jnp.concatenate([is_valid.reshape(N_MEMBER, width_all), jnp.zeros((N_MEMBER, BLOB_DEV), jnp.bool_)], 1)
    pad_within = jnp.concatenate([within.reshape(N_MEMBER, width_all), jnp.zeros((N_MEMBER, BLOB_DEV), jnp.int32)], 1)
    pad_member = jnp.concatenate([owner_member.reshape(N_MEMBER, width_all), jnp.zeros((N_MEMBER, BLOB_DEV), jnp.int32)], 1)
    sort_key = jnp.where(pad_valid, 0, 1).astype(jnp.int32)
    chosen = jnp.argsort(sort_key, axis=1, stable=True)[:, :BLOB_DEV]
    scores = jax.random.randint(shuffle_key, (N_MEMBER, BLOB_DEV), 0, 2 ** 19) * BLOB_DEV + jnp.arange(BLOB_DEV, dtype=jnp.int32)[None, :]
    shuffle = jnp.argsort(scores, axis=1)
    picked = jnp.take_along_axis(chosen, shuffle, axis=1)
    slot_valid = jnp.take_along_axis(pad_valid, picked, axis=1)
    slot_within = jnp.take_along_axis(pad_within, picked, axis=1)
    slot_member = jnp.take_along_axis(pad_member, picked, axis=1)
    owner_slot = jnp.clip(slot_member * PLAT_DEV + slot_within // PB, 0, PLAT_REG - 1)
    plate_ids = jnp.where(slot_valid, inverse_map[owner_slot], PLAT_REG).astype(jnp.int32)
    rank_ids = jnp.where(slot_valid, slot_within % PB, 0).astype(jnp.int32)
    return (plate_ids.reshape(REG_BLOBS), rank_ids.reshape(REG_BLOBS), owner_map)


def layout_tables(key):
    region_keys = jax.random.split(jax.random.fold_in(key, 7), N_REGION)
    plate_ids, rank_ids, owner_maps = jax.vmap(region_layout)(region_keys)
    return (plate_ids.reshape(NBLOBS), rank_ids.reshape(NBLOBS), owner_maps.reshape(NPLATS))


def draw_blob_platelet(key, part):
    return layout_tables(key)[0]


def draw_blob_rank(key, part):
    return layout_tables(key)[1]


def draw_platelet_owner(key, part):
    return layout_tables(key)[2]


def draw_positions(key, part):
    uniforms = jax.random.uniform(key, (3, NBLOBS), jnp.float32)
    region_index = (jnp.arange(NBLOBS) // REG_BLOBS).astype(jnp.float32)
    height = 1.0 + 3.0 * uniforms[2]
    along = (region_index + uniforms[0]) * slab_width
    across = uniforms[1] * span_width
    return jnp.stack([along, across, height], 0).astype(jnp.float32)


def draw_pair_list(key, part):
    local_tile = jnp.arange(NBLOCKS, dtype=jnp.int32) % REG_BLK
    self_index = local_tile + REG_BLK // 2
    scores = jax.random.randint(key, (NBLOCKS, EXT_BLK - 1), 0, 2 ** 19) * EXT_BLK + jnp.arange(EXT_BLK - 1, dtype=jnp.int32)[None, :]
    chosen = jnp.argsort(scores, axis=1)[:, :PAIRS - 1] + 1
    others = (self_index[:, None] + chosen) % EXT_BLK
    return jnp.concatenate([self_index[:, None], others], 1).astype(jnp.int32)


def draw_pair_count(key, part):
    first_key, second_key = jax.random.split(key, 2)
    counts = jax.random.randint(first_key, (NBLOCKS,), 1, PAIRS + 1)
    marked = jax.random.randint(second_key, (), 0, NBLOCKS)
    return jnp.where(jnp.arange(NBLOCKS) == marked, PAIRS, counts).astype(jnp.int32)


def levels(rng, shape, pieces, least, top_value):
    level, own = 1.0, jax.random.fold_in(rng, 6)
    for axis_at, blocks in pieces:
        heights = jnp.exp(jax.random.uniform(jax.random.fold_in(own, axis_at), (blocks,), jnp.float32, least / len(pieces), top_value / len(pieces)))
        level = level * jnp.repeat(heights, shape[axis_at] // blocks).reshape([-1 if axis == axis_at else 1 for axis in range(len(shape))])
    return level


def noise(key, shape, deviation, bound, cuts=(), kind=jnp.bfloat16):
    values = deviation * jax.random.normal(key, shape, jnp.float32)
    if cuts:
        values = values * levels(key, shape, cuts, -0.22, 0.18)
    return jnp.clip(values, -bound, bound).astype(kind)


def setup_inputs(seed: int = 0) -> dict:
    key_list = jax.random.split(jax.random.key(seed), 9)
    positions = draw_positions(jax.random.fold_in(key_list[8], 71), 0)
    forces = noise(key_list[1], (3, NBLOBS), 1.0, 6.0, ((1, 32),), jnp.float32)
    blob_platelet = draw_blob_platelet(jax.random.fold_in(key_list[8], 71), 0)
    blob_rank = draw_blob_rank(jax.random.fold_in(key_list[8], 71), 0)
    platelet_owner = draw_platelet_owner(jax.random.fold_in(key_list[8], 71), 0)
    pair_list = draw_pair_list(jax.random.fold_in(key_list[8], 71), 0)
    pair_count = draw_pair_count(jax.random.fold_in(key_list[8], 71), 0)
    preconditioner = noise(key_list[7], (NPLATS, BODY, BODY), BODY ** -0.5, 0.25, ((0, 32),))
    return dict(positions=positions, forces=forces, blob_platelet=blob_platelet, blob_rank=blob_rank, platelet_owner=platelet_owner, pair_list=pair_list, pair_count=pair_count, preconditioner=preconditioner)


soft_square = 1.0

def stokes_sum(targets, sources, pushes):
    force = pushes[:, :, None, :]
    separation = targets[:, :, :, None] - sources[:, :, None, :]
    dist_square = lax.optimization_barrier(jnp.sum(separation * separation, axis=0))
    force_along = lax.optimization_barrier(jnp.sum(separation * force, axis=0))
    kernel_weight = 1.0 / (8.0 * math.pi * (dist_square + soft_square) * jnp.sqrt(dist_square + soft_square))
    direct = ((dist_square + 2.0 * soft_square) * force + separation * force_along) * kernel_weight
    flip_source = jnp.array([1.0, 1.0, -1.0], jnp.float32)[:, None, None]
    flip_pair = jnp.array([1.0, 1.0, -1.0], jnp.float32)[:, None, None, None]
    unit_normal = jnp.array([0.0, 0.0, 1.0], jnp.float32)[:, None, None, None]
    height = sources[2][:, None, :]
    image_gap = targets[:, :, :, None] - (sources * flip_source)[:, :, None, :]
    image_square = lax.optimization_barrier(jnp.sum(image_gap * image_gap, axis=0))
    inverse_one = 1.0 / jnp.sqrt(image_square)
    inverse_three = inverse_one * inverse_one * inverse_one
    inverse_five = inverse_three * inverse_one * inverse_one
    image_along = lax.optimization_barrier(jnp.sum(image_gap * force, axis=0))
    mirrored = force * flip_pair
    mirror_along = lax.optimization_barrier(jnp.sum(image_gap * mirrored, axis=0))
    normal_gap = image_gap[2]
    stokes_image = force * inverse_one + image_gap * image_along * inverse_three
    doublet = height * (mirrored * inverse_three - 3.0 * image_gap * mirror_along * inverse_five)
    doublet = doublet + unit_normal * mirror_along * inverse_three
    doublet = doublet - (mirrored * normal_gap + image_gap * mirrored[2]) * inverse_three
    doublet = doublet + 3.0 * image_gap * normal_gap * mirror_along * inverse_five
    wall_term = (2.0 * height * doublet - stokes_image) * (1.0 / (8.0 * math.pi))
    return lax.optimization_barrier(jnp.sum(direct + wall_term, axis=3))

def reference(positions, forces, blob_platelet, blob_rank, platelet_owner, pair_list, pair_count, preconditioner):
    live_mask = (blob_platelet < PLAT_REG).astype(jnp.float32)
    pushes = forces * live_mask[None, :]
    slab_data = jnp.concatenate([positions, pushes], 0).reshape(6, N_REGION, REG_BLOBS)
    half_width = REG_BLOBS // 2
    zero_rim = jnp.zeros((6, 1, half_width), jnp.float32)
    lower_rim = jnp.concatenate([zero_rim, slab_data[:, :-1, half_width:]], 1)
    upper_rim = jnp.concatenate([slab_data[:, 1:, :half_width], zero_rim], 1)
    extended = jnp.concatenate([lower_rim, slab_data, upper_rim], 2)
    extended = extended.reshape(6, N_REGION, EXT_BLK, TILE).transpose(1, 0, 2, 3)
    region_pairs = pair_list.reshape(N_REGION, REG_BLK, PAIRS)
    region_counts = pair_count.reshape(N_REGION, REG_BLK)

    def region_velocity(region_items):
        ext_region, pair_rows, count_rows = region_items
        targets = ext_region[:3, REG_BLK // 2:REG_BLK // 2 + REG_BLK]
        accumulated = jnp.zeros((3, REG_BLK, TILE), jnp.float32)
        for pair_slot in range(PAIRS):
            picked = jnp.take(ext_region, pair_rows[:, pair_slot], axis=1)
            keep_mask = (pair_slot < count_rows).astype(jnp.float32)
            accumulated = accumulated + keep_mask[None, :, None] * stokes_sum(targets, picked[:3], picked[3:])
        return accumulated
    velocity = lax.map(region_velocity, (extended, region_pairs, region_counts))
    blob_velocity = velocity.transpose(1, 0, 2, 3).reshape(3, NBLOBS)
    owner_rows = platelet_owner.reshape(N_REGION, PLAT_REG)
    plate_rows = blob_platelet.reshape(N_REGION, REG_BLOBS)
    rank_rows = blob_rank.reshape(N_REGION, REG_BLOBS)
    safe_plate = jnp.minimum(plate_rows, PLAT_REG - 1).astype(jnp.int32)
    slot_of = jnp.take_along_axis(owner_rows, safe_plate, axis=1)
    body_index = jnp.where(plate_rows < PLAT_REG, slot_of * PB + rank_rows, PLAT_REG * PB).astype(jnp.int32)
    region_vel = blob_velocity.reshape(3, N_REGION, REG_BLOBS).transpose(1, 0, 2)

    def place_body(region_items):
        velocity_rows, index_rows = region_items
        return jnp.zeros((3, PLAT_REG * PB), jnp.float32).at[:, index_rows].set(velocity_rows, mode='drop')
    body_flat = lax.map(place_body, (region_vel, body_index))
    body_in = body_flat.reshape(N_REGION, 3, PLAT_REG, PB).transpose(0, 2, 1, 3).reshape(NPLATS, BODY)
    body_in = body_in.astype(jnp.bfloat16)

    def apply_block(block_items):
        return jnp.dot(block_items[0], block_items[1], preferred_element_type=jnp.float32)
    body_velocity = lax.map(apply_block, (preconditioner, body_in))
    return (blob_velocity, body_velocity)
```

```python
import functools
import math

import jax
import jax.numpy as jnp
from jax import lax
from jax.experimental import pallas as pl
from jax.experimental.pallas import tpu as pltpu
from jax.sharding import PartitionSpec as P

TILE = 128
SUB = 8
SCALE = 1.0 / (8.0 * math.pi)
MESH = pl.DeviceIdType.MESH


def pair_terms(x1, x2, x3, src):
    y1, y2, h, f1, f2, f3, h2 = src
    d1 = x1 - y1
    d2 = x2 - y2
    d3 = x3 - h
    r3 = x3 + h
    s = d1 * d1 + d2 * d2
    w = lax.rsqrt(s + d3 * d3 + 1.0)
    p = lax.rsqrt(s + r3 * r3)
    w3 = w * w * w
    p2 = p * p
    p3 = p2 * p
    along = d1 * f1 + d2 * f2
    full = along + d3 * f3
    mirror = along - r3 * f3
    cp3 = (h2 * x3) * p3
    alpha = (w + w3) - (p + cp3)
    gamma = 3.0 * (cp3 * p2) * mirror
    both = full * (w3 - p3) + gamma
    return (
        f1 * alpha + d1 * both,
        f2 * alpha + d2 * both,
        f3 * alpha + d3 * both + h2 * gamma,
    )


def kernel(
    n_region,
    n_member,
    pb,
    pos_hbm,
    force_hbm,
    plate_hbm,
    rank_hbm,
    owner_ref,
    list_ref,
    count_ref,
    pre_hbm,
    vel_out,
    body_out,
    pos,
    force,
    plate,
    rank,
    pre,
    ext,
    tgt,
    acc,
    vel,
    hot,
    in_sem,
    send_sem,
    recv_sem,
    vsend_sem,
    vrecv_sem,
):
    r = lax.axis_index("region")
    m = lax.axis_index("member")
    half = n_member // 2
    tiles = pos.shape[1] // TILE
    blobs = pos.shape[1]
    plates = owner_ref.shape[0]
    own_plates = pre.shape[0]
    pairs = list_ref.shape[1]
    has_low = r > 0
    has_high = r < n_region - 1
    to_high = jnp.logical_and(m >= half, has_high)
    to_low = jnp.logical_and(m < half, has_low)

    loads = [
        pltpu.make_async_copy(a, b, in_sem.at[i])
        for i, (a, b) in enumerate(
            ((pos_hbm, pos), (force_hbm, force), (plate_hbm, plate), (rank_hbm, rank), (pre_hbm, pre))
        )
    ]
    for load in loads:
        load.start()

    barrier = pltpu.get_barrier_semaphore()
    for step in range(1, n_member):
        pl.semaphore_signal(
            barrier, inc=1, device_id=(r, lax.rem(m + step, n_member)), device_id_type=MESH
        )

    @pl.when(has_low)
    def _():
        for k in range(half):
            pl.semaphore_signal(barrier, inc=1, device_id=(r - 1, half + k), device_id_type=MESH)

    @pl.when(has_high)
    def _():
        for k in range(half):
            pl.semaphore_signal(barrier, inc=1, device_id=(r + 1, k), device_id_type=MESH)

    for load in loads[:4]:
        load.wait()

    base = (half + m) * tiles
    plate_row = plate[...]
    rank_row = rank[...]
    live = plate_row < plates
    slot_of = jnp.zeros_like(plate_row)
    for k in range(plates):
        slot_of = jnp.where(plate_row == k, owner_ref[k], slot_of)
    body_at = jnp.where(live, slot_of * pb + rank_row, plates * pb).astype(jnp.float32)
    live_f = live.astype(jnp.float32)
    packed = jnp.concatenate(
        [pos[...], force[...] * live_f, body_at, jnp.zeros_like(body_at)], axis=0
    )
    for t in range(tiles):
        ext[base + t] = packed[:, t * TILE : (t + 1) * TILE]

    @pl.when(jnp.logical_not(has_low))
    def _():
        ext[pl.ds(0, half * tiles)] = jnp.zeros((half * tiles, SUB, TILE), jnp.float32)

    @pl.when(jnp.logical_not(has_high))
    def _():
        ext[pl.ds((half + n_member) * tiles, half * tiles)] = jnp.zeros(
            (half * tiles, SUB, TILE), jnp.float32
        )

    for t in range(tiles):
        for c in range(3):
            row = packed[c : c + 1, t * TILE : (t + 1) * TILE]
            tgt[t * 3 + c] = jnp.broadcast_to(row, (TILE, TILE)).T

    def block(e):
        return ext.at[pl.ds(e * tiles, tiles)]

    def near_copy(step):
        return pltpu.make_async_remote_copy(
            src_ref=block(half + m),
            dst_ref=block(half + m),
            send_sem=send_sem.at[step],
            recv_sem=recv_sem.at[half + m],
            device_id=(r, lax.rem(m + step, n_member)),
            device_id_type=MESH,
        )

    def rim_copy(k, shift, e):
        return pltpu.make_async_remote_copy(
            src_ref=block(half + m),
            dst_ref=block(e),
            send_sem=send_sem.at[n_member + k],
            recv_sem=recv_sem.at[e],
            device_id=(r + shift, lax.rem(m + k, n_member)),
            device_id_type=MESH,
        )

    def arrival(e):
        return pltpu.make_async_remote_copy(
            src_ref=block(e),
            dst_ref=block(e),
            send_sem=send_sem.at[0],
            recv_sem=recv_sem.at[e],
            device_id=(r, lax.rem(m + 1, n_member)),
            device_id_type=MESH,
        )

    rim_sends = jnp.where(jnp.logical_or(to_high, to_low), n_member, 0)
    pl.semaphore_wait(barrier, n_member - 1 + rim_sends)

    @pl.when(to_high)
    def _():
        for k in range(n_member):
            rim_copy(k, 1, m - half).start()

    @pl.when(to_low)
    def _():
        for k in range(n_member):
            rim_copy(k, -1, half + n_member + m).start()

    for step in range(1, n_member):
        near_copy(step).start()

    def one_pair(t, s, tile_id, first):
        keep = jnp.where(s < count_ref[t], SCALE, 0.0)
        rows = ext[tile_id]

        def wide(c):
            return jnp.broadcast_to(rows[c : c + 1], (SUB, TILE))

        h = wide(2)
        src = (wide(0), wide(1), h, wide(3) * keep, wide(4) * keep, wide(5) * keep, h + h)
        for b in range(TILE // SUB):
            at = pl.ds(b * SUB, SUB)
            terms = pair_terms(tgt[t * 3, at], tgt[t * 3 + 1, at], tgt[t * 3 + 2, at], src)
            for c in range(3):
                if first:
                    acc[t * 3 + c, at] = terms[c]
                else:
                    acc[t * 3 + c, at] = acc[t * 3 + c, at] + terms[c]

    @pl.loop(0, tiles)
    def _(t):
        one_pair(t, 0, base + t, True)

    for step in range(1, n_member):
        arrival(half + lax.rem(m + step, n_member)).wait_recv()

    @pl.when(has_low)
    def _():
        for k in range(half):
            arrival(k).wait_recv()

    @pl.when(has_high)
    def _():
        for k in range(half):
            arrival(half + n_member + k).wait_recv()

    @pl.loop(0, tiles * (pairs - 1))
    def _(i):
        t = i // (pairs - 1)
        s = i % (pairs - 1) + 1
        one_pair(t, s, list_ref[t, s], False)

    zeros = jnp.zeros((SUB - 3, TILE), jnp.float32)
    mine = pl.multiple_of(m * blobs, TILE)
    for t in range(tiles):
        rows = [jnp.sum(acc[t * 3 + c].T, axis=0, keepdims=True) for c in range(3)]
        at = pl.multiple_of(mine + t * TILE, TILE)
        vel[:, pl.ds(at, TILE)] = jnp.concatenate(rows + [zeros], axis=0)
        for c in range(3):
            vel_out[c : c + 1, t * TILE : (t + 1) * TILE] = rows[c]

    def vel_copy(step, at):
        part = vel.at[:, pl.ds(pl.multiple_of(at * blobs, TILE), blobs)]
        return pltpu.make_async_remote_copy(
            src_ref=part,
            dst_ref=part,
            send_sem=vsend_sem.at[step],
            recv_sem=vrecv_sem.at[at],
            device_id=(r, lax.rem(m + step, n_member)),
            device_id_type=MESH,
        )

    for step in range(1, n_member):
        vel_copy(step, m).start()

    width = hot.shape[0] // own_plates
    place = lax.broadcasted_iota(jnp.int32, (hot.shape[0], TILE), 0)

    @pl.loop(0, n_member * tiles)
    def _(i):
        local = ext[half * tiles + i][6:7].astype(jnp.int32) - m * (own_plates * pb)
        row = jnp.full_like(local, -1)
        for k in range(own_plates):
            inside = jnp.logical_and(local >= k * pb, local < (k + 1) * pb)
            row = jnp.where(inside, local + k * (width - pb), row)
        at = pl.multiple_of(i * TILE, TILE)
        hot[:, pl.ds(at, TILE)] = jnp.where(place == row, 1.0, 0.0).astype(jnp.bfloat16)

    loads[4].wait()
    for step in range(1, n_member):
        vel_copy(step, lax.rem(m + step, n_member)).wait_recv()

    placed = lax.dot_general(
        vel[...].astype(jnp.bfloat16),
        hot[...],
        (((1,), (1,)), ((), ())),
        preferred_element_type=jnp.float32,
    )
    order = pre.shape[2]
    total = 2 * width
    for k in range(own_plates):
        part = placed[:, k * width : (k + 1) * width]
        part = jnp.concatenate([part, jnp.zeros((SUB, total - width), jnp.float32)], axis=1)
        body = part[0:1]
        for c in range(1, 3):
            body = body + pltpu.roll(part, c * pb, 1)[c : c + 1]
        body_out[k : k + 1] = lax.dot_general(
            body[:, :order].astype(jnp.bfloat16),
            pre[k],
            (((1,), (1,)), ((), ())),
            preferred_element_type=jnp.float32,
        )

    for step in range(1, n_member):
        near_copy(step).wait_send()
        vel_copy(step, m).wait_send()

    @pl.when(to_high)
    def _():
        for k in range(n_member):
            rim_copy(k, 1, m - half).wait_send()

    @pl.when(to_low)
    def _():
        for k in range(n_member):
            rim_copy(k, -1, half + n_member + m).wait_send()


def on_device(n_region, n_member, positions, forces, blob_platelet, blob_rank, owner, pair_list, pair_count, pre):
    blobs = positions.shape[1]
    tiles = blobs // TILE
    own_plates, order, _ = pre.shape
    pb = order // 3
    width = -(-pb // TILE) * TILE
    anywhere = pl.BlockSpec(memory_space=pl.ANY)
    scalars = pl.BlockSpec(memory_space=pltpu.SMEM)
    vector = pl.BlockSpec(memory_space=pltpu.VMEM)
    return pl.pallas_call(
        functools.partial(kernel, n_region, n_member, pb),
        out_shape=(
            jax.ShapeDtypeStruct((3, blobs), jnp.float32),
            jax.ShapeDtypeStruct((own_plates, order), jnp.float32),
        ),
        in_specs=[anywhere] * 4 + [scalars] * 3 + [anywhere],
        out_specs=(vector, vector),
        scratch_shapes=[
            pltpu.VMEM((3, blobs), jnp.float32),
            pltpu.VMEM((3, blobs), jnp.float32),
            pltpu.VMEM((1, blobs), jnp.int32),
            pltpu.VMEM((1, blobs), jnp.int32),
            pltpu.VMEM(pre.shape, pre.dtype),
            pltpu.VMEM((2 * n_member * tiles, SUB, TILE), jnp.float32),
            pltpu.VMEM((3 * tiles, TILE, TILE), jnp.float32),
            pltpu.VMEM((3 * tiles, TILE, TILE), jnp.float32),
            pltpu.VMEM((SUB, n_member * blobs), jnp.float32),
            pltpu.VMEM((own_plates * width, n_member * blobs), jnp.bfloat16),
            pltpu.SemaphoreType.DMA((5,)),
            pltpu.SemaphoreType.DMA((2 * n_member,)),
            pltpu.SemaphoreType.DMA((2 * n_member,)),
            pltpu.SemaphoreType.DMA((n_member,)),
            pltpu.SemaphoreType.DMA((n_member,)),
        ],
        compiler_params=pltpu.CompilerParams(collective_id=0, has_side_effects=True),
    )(
        positions,
        forces,
        blob_platelet.reshape(1, blobs),
        blob_rank.reshape(1, blobs),
        owner,
        pair_list,
        pair_count,
        pre,
    )


def solution(mesh):
    placed = (
        P(None, ("region", "member")),
        P(None, ("region", "member")),
        P(("region", "member")),
        P(("region", "member")),
        P("region"),
        P(("region", "member"), None),
        P(("region", "member")),
        P(("region", "member"), None, None),
    )
    return jax.shard_map(
        functools.partial(on_device, mesh.shape["region"], mesh.shape["member"]),
        mesh=mesh,
        in_specs=placed,
        out_specs=(P(None, ("region", "member")), P(("region", "member"), None)),
        check_vma=False,
    )
```

```python
import functools
import math

import jax
import jax.numpy as jnp
from jax import lax
from jax.experimental import pallas as pl
from jax.experimental.pallas import tpu as pltpu
from jax.sharding import PartitionSpec as P

TILE = 128
SUB = 8
SCALE = 1.0 / (8.0 * math.pi)
MESH = pl.DeviceIdType.MESH


def pair_terms(x1, x2, x3, src):
    y1, y2, h, f1, f2, f3, h2 = src
    d1 = x1 - y1
    d2 = x2 - y2
    d3 = x3 - h
    r3 = x3 + h
    s = d1 * d1 + d2 * d2
    w = lax.rsqrt(s + d3 * d3 + 1.0)
    p = lax.rsqrt(s + r3 * r3)
    w3 = w * w * w
    p2 = p * p
    p3 = p2 * p
    along = d1 * f1 + d2 * f2
    full = along + d3 * f3
    mirror = along - r3 * f3
    cp3 = (h2 * x3) * p3
    alpha = (w + w3) - (p + cp3)
    gamma = 3.0 * (cp3 * p2) * mirror
    both = full * (w3 - p3) + gamma
    return (
        f1 * alpha + d1 * both,
        f2 * alpha + d2 * both,
        f3 * alpha + d3 * both + h2 * gamma,
    )


def kernel(
    n_region,
    n_member,
    pb,
    own_plates,
    pos_hbm,
    force_hbm,
    plate_hbm,
    rank_hbm,
    owner_hbm,
    list_hbm,
    count_hbm,
    vel_out,
    body_out,
    pos,
    force,
    plate,
    rank,
    owner_ref,
    list_ref,
    count_ref,
    ext,
    tgt,
    acc,
    vel,
    hot,
    in_sem,
    send_sem,
    recv_sem,
    vsend_sem,
    vrecv_sem,
):
    r = lax.axis_index("region")
    m = lax.axis_index("member")
    half = n_member // 2
    tiles = pos.shape[1] // TILE
    blobs = pos.shape[1]
    plates = owner_ref.shape[0]
    pairs = list_ref.shape[1]
    has_low = r > 0
    has_high = r < n_region - 1
    to_high = jnp.logical_and(m >= half, has_high)
    to_low = jnp.logical_and(m < half, has_low)

    loads = [
        pltpu.make_async_copy(a, b, in_sem.at[i])
        for i, (a, b) in enumerate(
            ((pos_hbm, pos), (force_hbm, force), (plate_hbm, plate.at[0]), (rank_hbm, rank.at[0]),
             (owner_hbm, owner_ref), (list_hbm, list_ref), (count_hbm, count_ref))
        )
    ]
    for load in loads:
        load.start()

    barrier = pltpu.get_barrier_semaphore()
    for step in range(1, n_member):
        pl.semaphore_signal(
            barrier, inc=1, device_id=(r, lax.rem(m + step, n_member)), device_id_type=MESH
        )

    @pl.when(has_low)
    def _():
        for k in range(half):
            pl.semaphore_signal(barrier, inc=1, device_id=(r - 1, half + k), device_id_type=MESH)

    @pl.when(has_high)
    def _():
        for k in range(half):
            pl.semaphore_signal(barrier, inc=1, device_id=(r + 1, k), device_id_type=MESH)

    for load in loads:
        load.wait()

    base = (half + m) * tiles
    plate_row = plate[...]
    rank_row = rank[...]
    live = plate_row < plates
    slot_of = jnp.zeros_like(plate_row)
    for k in range(plates):
        slot_of = jnp.where(plate_row == k, owner_ref[k], slot_of)
    body_at = jnp.where(live, slot_of * pb + rank_row, plates * pb).astype(jnp.float32)
    live_f = live.astype(jnp.float32)
    packed = jnp.concatenate(
        [pos[...], force[...] * live_f, body_at, jnp.zeros_like(body_at)], axis=0
    )
    for t in range(tiles):
        ext[base + t] = packed[:, t * TILE : (t + 1) * TILE]

    @pl.when(jnp.logical_not(has_low))
    def _():
        ext[pl.ds(0, half * tiles)] = jnp.zeros((half * tiles, SUB, TILE), jnp.float32)

    @pl.when(jnp.logical_not(has_high))
    def _():
        ext[pl.ds((half + n_member) * tiles, half * tiles)] = jnp.zeros(
            (half * tiles, SUB, TILE), jnp.float32
        )

    for t in range(tiles):
        for c in range(3):
            row = packed[c : c + 1, t * TILE : (t + 1) * TILE]
            tgt[t * 3 + c] = jnp.broadcast_to(row, (TILE, TILE)).T

    def block(e):
        return ext.at[pl.ds(e * tiles, tiles)]

    def near_copy(step):
        return pltpu.make_async_remote_copy(
            src_ref=block(half + m),
            dst_ref=block(half + m),
            send_sem=send_sem.at[step],
            recv_sem=recv_sem.at[half + m],
            device_id=(r, lax.rem(m + step, n_member)),
            device_id_type=MESH,
        )

    def rim_copy(k, shift, e):
        return pltpu.make_async_remote_copy(
            src_ref=block(half + m),
            dst_ref=block(e),
            send_sem=send_sem.at[n_member + k],
            recv_sem=recv_sem.at[e],
            device_id=(r + shift, lax.rem(m + k, n_member)),
            device_id_type=MESH,
        )

    def arrival(e):
        return pltpu.make_async_remote_copy(
            src_ref=block(e),
            dst_ref=block(e),
            send_sem=send_sem.at[0],
            recv_sem=recv_sem.at[e],
            device_id=(r, lax.rem(m + 1, n_member)),
            device_id_type=MESH,
        )

    rim_sends = jnp.where(jnp.logical_or(to_high, to_low), n_member, 0)
    pl.semaphore_wait(barrier, n_member - 1 + rim_sends)

    @pl.when(to_high)
    def _():
        for k in range(n_member):
            rim_copy(k, 1, m - half).start()

    @pl.when(to_low)
    def _():
        for k in range(n_member):
            rim_copy(k, -1, half + n_member + m).start()

    for step in range(1, n_member):
        near_copy(step).start()

    def one_pair(t, s, tile_id, first):
        keep = jnp.where(s < count_ref[t], SCALE, 0.0)
        rows = ext[tile_id]

        def wide(c):
            return jnp.broadcast_to(rows[c : c + 1], (SUB, TILE))

        h = wide(2)
        src = (wide(0), wide(1), h, wide(3) * keep, wide(4) * keep, wide(5) * keep, h + h)
        for b in range(TILE // SUB):
            at = pl.ds(b * SUB, SUB)
            terms = pair_terms(tgt[t * 3, at], tgt[t * 3 + 1, at], tgt[t * 3 + 2, at], src)
            for c in range(3):
                if first:
                    acc[t * 3 + c, at] = terms[c]
                else:
                    acc[t * 3 + c, at] = acc[t * 3 + c, at] + terms[c]

    @pl.loop(0, tiles)
    def _(t):
        one_pair(t, 0, base + t, True)

    for step in range(1, n_member):
        arrival(half + lax.rem(m + step, n_member)).wait_recv()

    @pl.when(has_low)
    def _():
        for k in range(half):
            arrival(k).wait_recv()

    @pl.when(has_high)
    def _():
        for k in range(half):
            arrival(half + n_member + k).wait_recv()

    @pl.loop(0, tiles * (pairs - 1))
    def _(i):
        t = i // (pairs - 1)
        s = i % (pairs - 1) + 1
        one_pair(t, s, list_ref[t, s], False)

    zeros = jnp.zeros((SUB - 3, TILE), jnp.float32)
    mine = pl.multiple_of(m * blobs, TILE)
    for t in range(tiles):
        rows = [jnp.sum(acc[t * 3 + c].T, axis=0, keepdims=True) for c in range(3)]
        at = pl.multiple_of(mine + t * TILE, TILE)
        vel[:, pl.ds(at, TILE)] = jnp.concatenate(rows + [zeros], axis=0)
        vel_out[:, t * TILE : (t + 1) * TILE] = jnp.concatenate(rows + [zeros], axis=0)

    def vel_copy(step, at):
        part = vel.at[:, pl.ds(pl.multiple_of(at * blobs, TILE), blobs)]
        return pltpu.make_async_remote_copy(
            src_ref=part,
            dst_ref=part,
            send_sem=vsend_sem.at[step],
            recv_sem=vrecv_sem.at[at],
            device_id=(r, lax.rem(m + step, n_member)),
            device_id_type=MESH,
        )

    for step in range(1, n_member):
        vel_copy(step, m).start()

    width = hot.shape[0] // own_plates
    place = lax.broadcasted_iota(jnp.int32, (hot.shape[0], TILE), 0)

    @pl.loop(0, n_member * tiles)
    def _(i):
        local = ext[half * tiles + i][6:7].astype(jnp.int32) - m * (own_plates * pb)
        row = jnp.full_like(local, -1)
        for k in range(own_plates):
            inside = jnp.logical_and(local >= k * pb, local < (k + 1) * pb)
            row = jnp.where(inside, local + k * (width - pb), row)
        at = pl.multiple_of(i * TILE, TILE)
        hot[:, pl.ds(at, TILE)] = jnp.where(place == row, 1.0, 0.0).astype(jnp.bfloat16)

    for step in range(1, n_member):
        vel_copy(step, lax.rem(m + step, n_member)).wait_recv()

    placed = lax.dot_general(
        vel[...].astype(jnp.bfloat16),
        hot[...],
        (((1,), (1,)), ((), ())),
        preferred_element_type=jnp.float32,
    )
    order = 3 * pb
    total = 2 * width
    for k in range(own_plates):
        part = placed[:, k * width : (k + 1) * width]
        part = jnp.concatenate([part, jnp.zeros((SUB, total - width), jnp.float32)], axis=1)
        body = part[0:1]
        for c in range(1, 3):
            body = body + pltpu.roll(part, c * pb, 1)[c : c + 1]
        body_out[k : k + 1] = body[:, :order]

    for step in range(1, n_member):
        near_copy(step).wait_send()
        vel_copy(step, m).wait_send()

    @pl.when(to_high)
    def _():
        for k in range(n_member):
            rim_copy(k, 1, m - half).wait_send()

    @pl.when(to_low)
    def _():
        for k in range(n_member):
            rim_copy(k, -1, half + n_member + m).wait_send()


def on_device(n_region, n_member, positions, forces, blob_platelet, blob_rank, owner, pair_list, pair_count, pre):
    blobs = positions.shape[1]
    tiles = blobs // TILE
    own_plates, order, _ = pre.shape
    pb = order // 3
    width = -(-pb // TILE) * TILE
    far = pl.BlockSpec(memory_space=pltpu.HBM)
    vector = pl.BlockSpec(memory_space=pltpu.VMEM)
    velocity, body_in = pl.pallas_call(
        functools.partial(kernel, n_region, n_member, pb, own_plates),
        out_shape=(
            pltpu.VMEM((SUB, blobs), jnp.float32),
            pltpu.VMEM((own_plates, order), jnp.float32),
        ),
        in_specs=[far] * 7,
        out_specs=(vector, vector),
        scratch_shapes=[
            pltpu.VMEM((3, blobs), jnp.float32),
            pltpu.VMEM((3, blobs), jnp.float32),
            pltpu.VMEM((1, blobs), jnp.int32),
            pltpu.VMEM((1, blobs), jnp.int32),
            pltpu.SMEM(owner.shape, jnp.int32),
            pltpu.SMEM(pair_list.shape, jnp.int32),
            pltpu.SMEM(pair_count.shape, jnp.int32),
            pltpu.VMEM((2 * n_member * tiles, SUB, TILE), jnp.float32),
            pltpu.VMEM((3 * tiles, TILE, TILE), jnp.float32),
            pltpu.VMEM((3 * tiles, TILE, TILE), jnp.float32),
            pltpu.VMEM((SUB, n_member * blobs), jnp.float32),
            pltpu.VMEM((own_plates * width, n_member * blobs), jnp.bfloat16),
            pltpu.SemaphoreType.DMA((7,)),
            pltpu.SemaphoreType.DMA((2 * n_member,)),
            pltpu.SemaphoreType.DMA((2 * n_member,)),
            pltpu.SemaphoreType.DMA((n_member,)),
            pltpu.SemaphoreType.DMA((n_member,)),
        ],
        compiler_params=pltpu.CompilerParams(collective_id=0, has_side_effects=True),
    )(
        positions,
        forces,
        blob_platelet,
        blob_rank,
        owner,
        pair_list,
        pair_count,
    )
    body_velocity = jnp.einsum(
        "pab,pb->pa", pre, body_in.astype(jnp.bfloat16), preferred_element_type=jnp.float32
    )
    return velocity[:3], body_velocity


def solution(mesh):
    placed = (
        P(None, ("region", "member")),
        P(None, ("region", "member")),
        P(("region", "member")),
        P(("region", "member")),
        P("region"),
        P(("region", "member"), None),
        P(("region", "member")),
        P(("region", "member"), None, None),
    )
    return jax.shard_map(
        functools.partial(on_device, mesh.shape["region"], mesh.shape["member"]),
        mesh=mesh,
        in_specs=placed,
        out_specs=(P(None, ("region", "member")), P(("region", "member"), None)),
        check_vma=False,
    )
```

```python
import functools
import math

import jax
import jax.numpy as jnp
from jax import lax
from jax.experimental import pallas as pl
from jax.experimental.pallas import tpu as pltpu
from jax.sharding import PartitionSpec as P

TILE = 128
SUB = 8
VROWS = 4
SCALE = 1.0 / (8.0 * math.pi)
MESH = pl.DeviceIdType.MESH


def pair_terms(x1, x2, x3, src):
    y1, y2, h, f1, f2, f3, h2 = src
    d1 = x1 - y1
    d2 = x2 - y2
    d3 = x3 - h
    r3 = x3 + h
    s = d1 * d1 + d2 * d2
    w = lax.rsqrt(s + d3 * d3 + 1.0)
    p = lax.rsqrt(s + r3 * r3)
    w3 = w * w * w
    p2 = p * p
    p3 = p2 * p
    along = d1 * f1 + d2 * f2
    full = along + d3 * f3
    mirror = along - r3 * f3
    cp3 = (h2 * x3) * p3
    alpha = (w + w3) - (p + cp3)
    gamma = 3.0 * (cp3 * p2) * mirror
    both = full * (w3 - p3) + gamma
    return (
        f1 * alpha + d1 * both,
        f2 * alpha + d2 * both,
        f3 * alpha + d3 * both + h2 * gamma,
    )


def kernel(
    n_region,
    n_member,
    pb,
    own_plates,
    pos_hbm,
    force_hbm,
    plate_hbm,
    rank_hbm,
    owner_hbm,
    list_hbm,
    count_hbm,
    vel_out,
    body_out,
    pos,
    force,
    plate,
    rank,
    owner_ref,
    list_ref,
    count_ref,
    ext,
    tgt,
    acc,
    vel,
    hot,
    in_sem,
    send_sem,
    recv_sem,
    vsend_sem,
    vrecv_sem,
):
    r = lax.axis_index("region")
    m = lax.axis_index("member")
    half = n_member // 2
    tiles = pos.shape[1] // TILE
    blobs = pos.shape[1]
    plates = owner_ref.shape[0]
    pairs = list_ref.shape[1]
    has_low = r > 0
    has_high = r < n_region - 1
    to_high = jnp.logical_and(m >= half, has_high)
    to_low = jnp.logical_and(m < half, has_low)

    loads = [
        pltpu.make_async_copy(a, b, in_sem.at[i])
        for i, (a, b) in enumerate(
            ((pos_hbm, pos), (force_hbm, force), (plate_hbm, plate.at[0]), (rank_hbm, rank.at[0]),
             (owner_hbm, owner_ref), (list_hbm, list_ref), (count_hbm, count_ref))
        )
    ]
    for load in loads:
        load.start()

    barrier = pltpu.get_barrier_semaphore()
    for step in range(1, n_member):
        pl.semaphore_signal(
            barrier, inc=1, device_id=(r, lax.rem(m + step, n_member)), device_id_type=MESH
        )

    @pl.when(has_low)
    def _():
        for k in range(half):
            pl.semaphore_signal(barrier, inc=1, device_id=(r - 1, half + k), device_id_type=MESH)

    @pl.when(has_high)
    def _():
        for k in range(half):
            pl.semaphore_signal(barrier, inc=1, device_id=(r + 1, k), device_id_type=MESH)

    for load in loads:
        load.wait()

    base = (half + m) * tiles
    plate_row = plate[...]
    rank_row = rank[...]
    live = plate_row < plates
    slot_of = jnp.zeros_like(plate_row)
    for k in range(plates):
        slot_of = jnp.where(plate_row == k, owner_ref[k], slot_of)
    body_at = jnp.where(live, slot_of * pb + rank_row, plates * pb).astype(jnp.float32)
    live_f = live.astype(jnp.float32)
    packed = jnp.concatenate(
        [pos[...], force[...] * live_f, body_at, jnp.zeros_like(body_at)], axis=0
    )
    for t in range(tiles):
        ext[base + t] = packed[:, t * TILE : (t + 1) * TILE]

    @pl.when(jnp.logical_not(has_low))
    def _():
        ext[pl.ds(0, half * tiles)] = jnp.zeros((half * tiles, SUB, TILE), jnp.float32)

    @pl.when(jnp.logical_not(has_high))
    def _():
        ext[pl.ds((half + n_member) * tiles, half * tiles)] = jnp.zeros(
            (half * tiles, SUB, TILE), jnp.float32
        )

    for t in range(tiles):
        for c in range(3):
            row = packed[c : c + 1, t * TILE : (t + 1) * TILE]
            tgt[t * 3 + c] = jnp.broadcast_to(row, (TILE, TILE)).T

    def block(e):
        return ext.at[pl.ds(e * tiles, tiles)]

    def near_copy(step):
        return pltpu.make_async_remote_copy(
            src_ref=block(half + m),
            dst_ref=block(half + m),
            send_sem=send_sem.at[step],
            recv_sem=recv_sem.at[half + m],
            device_id=(r, lax.rem(m + step, n_member)),
            device_id_type=MESH,
        )

    def rim_copy(k, shift, e):
        return pltpu.make_async_remote_copy(
            src_ref=block(half + m),
            dst_ref=block(e),
            send_sem=send_sem.at[n_member + k],
            recv_sem=recv_sem.at[e],
            device_id=(r + shift, lax.rem(m + k, n_member)),
            device_id_type=MESH,
        )

    def arrival(e):
        return pltpu.make_async_remote_copy(
            src_ref=block(e),
            dst_ref=block(e),
            send_sem=send_sem.at[0],
            recv_sem=recv_sem.at[e],
            device_id=(r, lax.rem(m + 1, n_member)),
            device_id_type=MESH,
        )

    rim_sends = jnp.where(jnp.logical_or(to_high, to_low), n_member, 0)
    pl.semaphore_wait(barrier, n_member - 1 + rim_sends)

    @pl.when(to_high)
    def _():
        for k in range(n_member):
            rim_copy(k, 1, m - half).start()

    @pl.when(to_low)
    def _():
        for k in range(n_member):
            rim_copy(k, -1, half + n_member + m).start()

    for step in range(1, n_member):
        near_copy(step).start()

    def one_pair(t, s, tile_id, first):
        keep = jnp.where(s < count_ref[t], SCALE, 0.0)
        rows = ext[tile_id]

        def wide(c):
            return jnp.broadcast_to(rows[c : c + 1], (SUB, TILE))

        h = wide(2)
        src = (wide(0), wide(1), h, wide(3) * keep, wide(4) * keep, wide(5) * keep, h + h)
        for b in range(TILE // SUB):
            at = pl.ds(b * SUB, SUB)
            terms = pair_terms(tgt[t * 3, at], tgt[t * 3 + 1, at], tgt[t * 3 + 2, at], src)
            for c in range(3):
                if first:
                    acc[t * 3 + c, at] = terms[c]
                else:
                    acc[t * 3 + c, at] = acc[t * 3 + c, at] + terms[c]

    @pl.loop(0, tiles)
    def _(t):
        one_pair(t, 0, base + t, True)

    for step in range(1, n_member):
        arrival(half + lax.rem(m + step, n_member)).wait_recv()

    @pl.when(has_low)
    def _():
        for k in range(half):
            arrival(k).wait_recv()

    @pl.when(has_high)
    def _():
        for k in range(half):
            arrival(half + n_member + k).wait_recv()

    zeros = jnp.zeros((VROWS - 3, TILE), jnp.float32)

    def vel_copy(t, step, at):
        part = vel.at[:, pl.ds(pl.multiple_of(at * blobs + t * TILE, TILE), TILE)]
        return pltpu.make_async_remote_copy(
            src_ref=part,
            dst_ref=part,
            send_sem=vsend_sem.at[t, step],
            recv_sem=vrecv_sem.at[t, at],
            device_id=(r, lax.rem(m + step, n_member)),
            device_id_type=MESH,
        )

    for t in range(tiles):

        @pl.loop(1, pairs)
        def _(s):
            one_pair(t, s, list_ref[t, s], False)

        rows = [jnp.sum(acc[t * 3 + c].T, axis=0, keepdims=True) for c in range(3)]
        at = pl.multiple_of(m * blobs + t * TILE, TILE)
        vel[:, pl.ds(at, TILE)] = jnp.concatenate(rows + [zeros], axis=0)
        vel_out[:, t * TILE : (t + 1) * TILE] = jnp.concatenate(rows, axis=0)
        for step in range(1, n_member):
            vel_copy(t, step, m).start()

    width = hot.shape[0] // own_plates
    place = lax.broadcasted_iota(jnp.int32, (hot.shape[0], TILE), 0)

    @pl.loop(0, n_member * tiles)
    def _(i):
        local = ext[half * tiles + i][6:7].astype(jnp.int32) - m * (own_plates * pb)
        row = jnp.full_like(local, -1)
        for k in range(own_plates):
            inside = jnp.logical_and(local >= k * pb, local < (k + 1) * pb)
            row = jnp.where(inside, local + k * (width - pb), row)
        at = pl.multiple_of(i * TILE, TILE)
        hot[:, pl.ds(at, TILE)] = jnp.where(place == row, 1.0, 0.0).astype(jnp.bfloat16)

    for step in range(1, n_member):
        for t in range(tiles):
            vel_copy(t, step, lax.rem(m + step, n_member)).wait_recv()

    placed = lax.dot_general(
        vel[...].astype(jnp.bfloat16),
        hot[...],
        (((1,), (1,)), ((), ())),
        preferred_element_type=jnp.float32,
    )
    order = 3 * pb
    total = 2 * width
    for k in range(own_plates):
        part = placed[:, k * width : (k + 1) * width]
        part = jnp.concatenate([part, jnp.zeros((VROWS, total - width), jnp.float32)], axis=1)
        body = part[0:1]
        for c in range(1, 3):
            body = body + pltpu.roll(part, c * pb, 1)[c : c + 1]
        body_out[k : k + 1] = body[:, :order]

    for step in range(1, n_member):
        near_copy(step).wait_send()
        for t in range(tiles):
            vel_copy(t, step, m).wait_send()

    @pl.when(to_high)
    def _():
        for k in range(n_member):
            rim_copy(k, 1, m - half).wait_send()

    @pl.when(to_low)
    def _():
        for k in range(n_member):
            rim_copy(k, -1, half + n_member + m).wait_send()


def on_device(n_region, n_member, positions, forces, blob_platelet, blob_rank, owner, pair_list, pair_count, pre):
    blobs = positions.shape[1]
    tiles = blobs // TILE
    own_plates, order, _ = pre.shape
    pb = order // 3
    width = -(-pb // TILE) * TILE
    far = pl.BlockSpec(memory_space=pltpu.HBM)
    vector = pl.BlockSpec(memory_space=pltpu.VMEM)
    velocity, body_in = pl.pallas_call(
        functools.partial(kernel, n_region, n_member, pb, own_plates),
        out_shape=(
            pltpu.VMEM((3, blobs), jnp.float32),
            pltpu.VMEM((own_plates, order), jnp.float32),
        ),
        in_specs=[far] * 7,
        out_specs=(vector, vector),
        scratch_shapes=[
            pltpu.VMEM((3, blobs), jnp.float32),
            pltpu.VMEM((3, blobs), jnp.float32),
            pltpu.VMEM((1, blobs), jnp.int32),
            pltpu.VMEM((1, blobs), jnp.int32),
            pltpu.SMEM(owner.shape, jnp.int32),
            pltpu.SMEM(pair_list.shape, jnp.int32),
            pltpu.SMEM(pair_count.shape, jnp.int32),
            pltpu.VMEM((2 * n_member * tiles, SUB, TILE), jnp.float32),
            pltpu.VMEM((3 * tiles, TILE, TILE), jnp.float32),
            pltpu.VMEM((3 * tiles, TILE, TILE), jnp.float32),
            pltpu.VMEM((VROWS, n_member * blobs), jnp.float32),
            pltpu.VMEM((own_plates * width, n_member * blobs), jnp.bfloat16),
            pltpu.SemaphoreType.DMA((7,)),
            pltpu.SemaphoreType.DMA((2 * n_member,)),
            pltpu.SemaphoreType.DMA((2 * n_member,)),
            pltpu.SemaphoreType.DMA((tiles, n_member)),
            pltpu.SemaphoreType.DMA((tiles, n_member)),
        ],
        compiler_params=pltpu.CompilerParams(collective_id=0, has_side_effects=True),
    )(
        positions,
        forces,
        blob_platelet,
        blob_rank,
        owner,
        pair_list,
        pair_count,
    )
    body_velocity = jnp.einsum(
        "pab,pb->pa", pre, body_in.astype(jnp.bfloat16), preferred_element_type=jnp.float32
    )
    return velocity, body_velocity


def solution(mesh):
    placed = (
        P(None, ("region", "member")),
        P(None, ("region", "member")),
        P(("region", "member")),
        P(("region", "member")),
        P("region"),
        P(("region", "member"), None),
        P(("region", "member")),
        P(("region", "member"), None, None),
    )
    return jax.shard_map(
        functools.partial(on_device, mesh.shape["region"], mesh.shape["member"]),
        mesh=mesh,
        in_specs=placed,
        out_specs=(P(None, ("region", "member")), P(("region", "member"), None)),
        check_vma=False,
    )
```

```python
import functools
import math

import jax
import jax.numpy as jnp
from jax import lax
from jax.experimental import pallas as pl
from jax.experimental.pallas import tpu as pltpu
from jax.sharding import PartitionSpec as P

TILE = 128
SUB = 8
VROWS = 4
SCALE = 1.0 / (8.0 * math.pi)
MESH = pl.DeviceIdType.MESH


def pair_terms(x1, x2, x3, src):
    y1, y2, h, f1, f2, f3, h2 = src
    d1 = x1 - y1
    d2 = x2 - y2
    d3 = x3 - h
    r3 = x3 + h
    s = d1 * d1 + d2 * d2
    w = lax.rsqrt(s + d3 * d3 + 1.0)
    p = lax.rsqrt(s + r3 * r3)
    w3 = w * w * w
    p2 = p * p
    p3 = p2 * p
    along = d1 * f1 + d2 * f2
    full = along + d3 * f3
    mirror = along - r3 * f3
    cp3 = (h2 * x3) * p3
    alpha = (w + w3) - (p + cp3)
    gamma = 3.0 * (cp3 * p2) * mirror
    both = full * (w3 - p3) + gamma
    return (
        f1 * alpha + d1 * both,
        f2 * alpha + d2 * both,
        f3 * alpha + d3 * both + h2 * gamma,
    )


def kernel(
    n_region,
    n_member,
    pb,
    own_plates,
    pos_hbm,
    force_hbm,
    plate_hbm,
    rank_hbm,
    owner_hbm,
    list_hbm,
    count_hbm,
    vel_out,
    body_out,
    pos,
    force,
    plate,
    rank,
    owner_ref,
    list_ref,
    count_ref,
    ext,
    tgt,
    acc,
    vel,
    hot,
    in_sem,
    send_sem,
    recv_sem,
    vsend_sem,
    vrecv_sem,
):
    r = lax.axis_index("region")
    m = lax.axis_index("member")
    half = n_member // 2
    tiles = pos.shape[1] // TILE
    blobs = pos.shape[1]
    plates = owner_ref.shape[0]
    pairs = list_ref.shape[1]
    has_low = r > 0
    has_high = r < n_region - 1
    to_high = jnp.logical_and(m >= half, has_high)
    to_low = jnp.logical_and(m < half, has_low)

    loads = [
        pltpu.make_async_copy(a, b, in_sem.at[i])
        for i, (a, b) in enumerate(
            ((pos_hbm, pos), (force_hbm, force), (plate_hbm, plate.at[0]), (rank_hbm, rank.at[0]),
             (owner_hbm, owner_ref), (list_hbm, list_ref), (count_hbm, count_ref))
        )
    ]
    for load in loads:
        load.start()

    barrier = pltpu.get_barrier_semaphore()
    for step in range(1, n_member):
        pl.semaphore_signal(
            barrier, inc=1, device_id=(r, lax.rem(m + step, n_member)), device_id_type=MESH
        )

    @pl.when(has_low)
    def _():
        for k in range(half):
            pl.semaphore_signal(barrier, inc=1, device_id=(r - 1, half + k), device_id_type=MESH)

    @pl.when(has_high)
    def _():
        for k in range(half):
            pl.semaphore_signal(barrier, inc=1, device_id=(r + 1, k), device_id_type=MESH)

    for load in loads:
        load.wait()

    base = (half + m) * tiles
    plate_row = plate[...]
    rank_row = rank[...]
    live = plate_row < plates
    slot_of = jnp.zeros_like(plate_row)
    for k in range(plates):
        slot_of = jnp.where(plate_row == k, owner_ref[k], slot_of)
    body_at = jnp.where(live, slot_of * pb + rank_row, plates * pb).astype(jnp.float32)
    live_f = live.astype(jnp.float32)
    packed = jnp.concatenate(
        [pos[...], force[...] * live_f, body_at, jnp.zeros_like(body_at)], axis=0
    )
    for t in range(tiles):
        ext[base + t] = packed[:, t * TILE : (t + 1) * TILE]

    @pl.when(jnp.logical_not(has_low))
    def _():
        ext[pl.ds(0, half * tiles)] = jnp.zeros((half * tiles, SUB, TILE), jnp.float32)

    @pl.when(jnp.logical_not(has_high))
    def _():
        ext[pl.ds((half + n_member) * tiles, half * tiles)] = jnp.zeros(
            (half * tiles, SUB, TILE), jnp.float32
        )

    for t in range(tiles):
        for c in range(3):
            row = packed[c : c + 1, t * TILE : (t + 1) * TILE]
            tgt[t * 3 + c] = jnp.broadcast_to(row, (TILE, TILE)).T

    def block(e):
        return ext.at[pl.ds(e * tiles, tiles)]

    def near_copy(step):
        return pltpu.make_async_remote_copy(
            src_ref=block(half + m),
            dst_ref=block(half + m),
            send_sem=send_sem.at[step],
            recv_sem=recv_sem.at[half + m],
            device_id=(r, lax.rem(m + step, n_member)),
            device_id_type=MESH,
        )

    def rim_copy(k, shift, e):
        return pltpu.make_async_remote_copy(
            src_ref=block(half + m),
            dst_ref=block(e),
            send_sem=send_sem.at[n_member + k],
            recv_sem=recv_sem.at[e],
            device_id=(r + shift, lax.rem(m + k, n_member)),
            device_id_type=MESH,
        )

    def arrival(e):
        return pltpu.make_async_remote_copy(
            src_ref=block(e),
            dst_ref=block(e),
            send_sem=send_sem.at[0],
            recv_sem=recv_sem.at[e],
            device_id=(r, lax.rem(m + 1, n_member)),
            device_id_type=MESH,
        )

    rim_sends = jnp.where(jnp.logical_or(to_high, to_low), n_member, 0)
    pl.semaphore_wait(barrier, n_member - 1 + rim_sends)

    @pl.when(to_high)
    def _():
        for k in range(n_member):
            rim_copy(k, 1, m - half).start()

    @pl.when(to_low)
    def _():
        for k in range(n_member):
            rim_copy(k, -1, half + n_member + m).start()

    for step in range(1, n_member):
        near_copy(step).start()

    def one_pair(t, s, tile_id, first):
        keep = jnp.where(s < count_ref[t], SCALE, 0.0)
        rows = ext[tile_id]

        def wide(c):
            return jnp.broadcast_to(rows[c : c + 1], (SUB, TILE))

        h = wide(2)
        src = (wide(0), wide(1), h, wide(3) * keep, wide(4) * keep, wide(5) * keep, h + h)
        for b in range(TILE // SUB):
            at = pl.ds(b * SUB, SUB)
            terms = pair_terms(tgt[t * 3, at], tgt[t * 3 + 1, at], tgt[t * 3 + 2, at], src)
            for c in range(3):
                if first:
                    acc[t * 3 + c, at] = terms[c]
                else:
                    acc[t * 3 + c, at] = acc[t * 3 + c, at] + terms[c]

    @pl.loop(0, tiles)
    def _(t):
        one_pair(t, 0, base + t, True)

    for step in range(1, n_member):
        arrival(half + lax.rem(m + step, n_member)).wait_recv()

    @pl.when(has_low)
    def _():
        for k in range(half):
            arrival(k).wait_recv()

    @pl.when(has_high)
    def _():
        for k in range(half):
            arrival(half + n_member + k).wait_recv()

    zeros = jnp.zeros((VROWS - 3, TILE), jnp.float32)

    def vel_copy(t, step, at):
        part = vel.at[:, pl.ds(pl.multiple_of(at * blobs + t * TILE, TILE), TILE)]
        return pltpu.make_async_remote_copy(
            src_ref=part,
            dst_ref=part,
            send_sem=vsend_sem.at[t, step],
            recv_sem=vrecv_sem.at[t, at],
            device_id=(r, lax.rem(m + step, n_member)),
            device_id_type=MESH,
        )

    for t in range(tiles):

        @pl.loop(1, pairs)
        def _(s):
            one_pair(t, s, list_ref[t, s], False)

        rows = [jnp.sum(acc[t * 3 + c].T, axis=0, keepdims=True) for c in range(3)]
        at = pl.multiple_of(m * blobs + t * TILE, TILE)
        vel[:, pl.ds(at, TILE)] = jnp.concatenate(rows + [zeros], axis=0)
        vel_out[:, t * TILE : (t + 1) * TILE] = jnp.concatenate(rows, axis=0)
        for step in range(1, n_member):
            vel_copy(t, step, m).start()

    width = hot.shape[0] // own_plates
    place = lax.broadcasted_iota(jnp.int32, (hot.shape[0], TILE), 0)

    @pl.loop(0, n_member * tiles)
    def _(i):
        local = ext[half * tiles + i][6:7].astype(jnp.int32) - m * (own_plates * pb)
        row = jnp.full_like(local, -1)
        for k in range(own_plates):
            inside = jnp.logical_and(local >= k * pb, local < (k + 1) * pb)
            row = jnp.where(inside, local + k * (width - pb), row)
        at = pl.multiple_of(i * TILE, TILE)
        hot[:, pl.ds(at, TILE)] = jnp.where(place == row, 1.0, 0.0).astype(jnp.bfloat16)

    for step in range(1, n_member):
        for t in range(tiles):
            vel_copy(t, step, lax.rem(m + step, n_member)).wait_recv()

    placed = lax.dot_general(
        vel[...].astype(jnp.bfloat16),
        hot[...],
        (((1,), (1,)), ((), ())),
        preferred_element_type=jnp.float32,
    )
    order = 3 * pb
    total = 2 * width
    for k in range(own_plates):
        part = placed[:, k * width : (k + 1) * width]
        part = jnp.concatenate([part, jnp.zeros((VROWS, total - width), jnp.float32)], axis=1)
        body = part[0:1]
        for c in range(1, 3):
            body = body + pltpu.roll(part, c * pb, 1)[c : c + 1]
        body_out[k : k + 1] = body[:, :order]

    for step in range(1, n_member):
        near_copy(step).wait_send()
        for t in range(tiles):
            vel_copy(t, step, m).wait_send()

    @pl.when(to_high)
    def _():
        for k in range(n_member):
            rim_copy(k, 1, m - half).wait_send()

    @pl.when(to_low)
    def _():
        for k in range(n_member):
            rim_copy(k, -1, half + n_member + m).wait_send()


def finish(vel_ref, body_ref, vel_out, body_out):
    vel_out[...] = vel_ref[...]
    body_out[...] = body_ref[...]


def on_device(n_region, n_member, positions, forces, blob_platelet, blob_rank, owner, pair_list, pair_count, pre):
    blobs = positions.shape[1]
    tiles = blobs // TILE
    own_plates, order, _ = pre.shape
    pb = order // 3
    width = -(-pb // TILE) * TILE
    far = pl.BlockSpec(memory_space=pltpu.HBM)
    vector = pl.BlockSpec(memory_space=pltpu.VMEM)
    velocity, body_in = pl.pallas_call(
        functools.partial(kernel, n_region, n_member, pb, own_plates),
        out_shape=(
            pltpu.VMEM((3, blobs), jnp.float32),
            pltpu.VMEM((own_plates, order), jnp.float32),
        ),
        in_specs=[far] * 7,
        out_specs=(vector, vector),
        scratch_shapes=[
            pltpu.VMEM((3, blobs), jnp.float32),
            pltpu.VMEM((3, blobs), jnp.float32),
            pltpu.VMEM((1, blobs), jnp.int32),
            pltpu.VMEM((1, blobs), jnp.int32),
            pltpu.SMEM(owner.shape, jnp.int32),
            pltpu.SMEM(pair_list.shape, jnp.int32),
            pltpu.SMEM(pair_count.shape, jnp.int32),
            pltpu.VMEM((2 * n_member * tiles, SUB, TILE), jnp.float32),
            pltpu.VMEM((3 * tiles, TILE, TILE), jnp.float32),
            pltpu.VMEM((3 * tiles, TILE, TILE), jnp.float32),
            pltpu.VMEM((VROWS, n_member * blobs), jnp.float32),
            pltpu.VMEM((own_plates * width, n_member * blobs), jnp.bfloat16),
            pltpu.SemaphoreType.DMA((7,)),
            pltpu.SemaphoreType.DMA((2 * n_member,)),
            pltpu.SemaphoreType.DMA((2 * n_member,)),
            pltpu.SemaphoreType.DMA((tiles, n_member)),
            pltpu.SemaphoreType.DMA((tiles, n_member)),
        ],
        compiler_params=pltpu.CompilerParams(collective_id=0, has_side_effects=True),
    )(
        positions,
        forces,
        blob_platelet,
        blob_rank,
        owner,
        pair_list,
        pair_count,
    )
    body_velocity = jnp.einsum(
        "pab,pb->pa", pre, body_in.astype(jnp.bfloat16), preferred_element_type=jnp.float32
    )
    return pl.pallas_call(
        finish,
        out_shape=(
            jax.ShapeDtypeStruct(velocity.shape, jnp.float32),
            jax.ShapeDtypeStruct(body_velocity.shape, jnp.float32),
        ),
        in_specs=[vector, vector],
        out_specs=(vector, vector),
        compiler_params=pltpu.CompilerParams(vmem_limit_bytes=1024 * 1024),
    )(velocity, body_velocity)


def solution(mesh):
    placed = (
        P(None, ("region", "member")),
        P(None, ("region", "member")),
        P(("region", "member")),
        P(("region", "member")),
        P("region"),
        P(("region", "member"), None),
        P(("region", "member")),
        P(("region", "member"), None, None),
    )
    return jax.shard_map(
        functools.partial(on_device, mesh.shape["region"], mesh.shape["member"]),
        mesh=mesh,
        in_specs=placed,
        out_specs=(P(None, ("region", "member")), P(("region", "member"), None)),
        check_vma=False,
    )
```

```python
import functools
import math

import jax
import jax.numpy as jnp
from jax import lax
from jax.experimental import pallas as pl
from jax.experimental.pallas import tpu as pltpu
from jax.sharding import PartitionSpec as P

TILE = 128
SUB = 8
VROWS = 4
SCALE = 1.0 / (8.0 * math.pi)
MESH = pl.DeviceIdType.MESH


def pair_terms(x1, x2, x3, src):
    y1, y2, h, f1, f2, f3, h2 = src
    d1 = x1 - y1
    d2 = x2 - y2
    d3 = x3 - h
    r3 = x3 + h
    s = d1 * d1 + d2 * d2
    w = lax.rsqrt(s + d3 * d3 + 1.0)
    p = lax.rsqrt(s + r3 * r3)
    w3 = w * w * w
    p2 = p * p
    p3 = p2 * p
    along = d1 * f1 + d2 * f2
    full = along + d3 * f3
    mirror = along - r3 * f3
    cp3 = (h2 * x3) * p3
    alpha = (w + w3) - (p + cp3)
    gamma = 3.0 * (cp3 * p2) * mirror
    both = full * (w3 - p3) + gamma
    return (
        f1 * alpha + d1 * both,
        f2 * alpha + d2 * both,
        f3 * alpha + d3 * both + h2 * gamma,
    )


def kernel(
    n_region,
    n_member,
    pb,
    own_plates,
    pos_hbm,
    force_hbm,
    plate_hbm,
    rank_hbm,
    owner_hbm,
    list_hbm,
    count_hbm,
    vel_out,
    body_out,
    pos,
    force,
    plate,
    rank,
    owner_ref,
    list_ref,
    count_ref,
    ext,
    tgt,
    acc,
    vel,
    hot,
    in_sem,
    send_sem,
    recv_sem,
    vsend_sem,
    vrecv_sem,
):
    r = lax.axis_index("region")
    m = lax.axis_index("member")
    half = n_member // 2
    tiles = pos.shape[1] // TILE
    blobs = pos.shape[1]
    plates = owner_ref.shape[0]
    pairs = list_ref.shape[1]
    has_low = r > 0
    has_high = r < n_region - 1
    to_high = jnp.logical_and(m >= half, has_high)
    to_low = jnp.logical_and(m < half, has_low)

    loads = [
        pltpu.make_async_copy(a, b, in_sem.at[i])
        for i, (a, b) in enumerate(
            ((pos_hbm, pos), (force_hbm, force), (plate_hbm, plate.at[0]), (rank_hbm, rank.at[0]),
             (owner_hbm, owner_ref), (list_hbm, list_ref), (count_hbm, count_ref))
        )
    ]
    for load in loads:
        load.start()

    barrier = pltpu.get_barrier_semaphore()
    for step in range(1, n_member):
        pl.semaphore_signal(
            barrier, inc=1, device_id=(r, lax.rem(m + step, n_member)), device_id_type=MESH
        )

    @pl.when(has_low)
    def _():
        for k in range(half):
            pl.semaphore_signal(barrier, inc=1, device_id=(r - 1, half + k), device_id_type=MESH)

    @pl.when(has_high)
    def _():
        for k in range(half):
            pl.semaphore_signal(barrier, inc=1, device_id=(r + 1, k), device_id_type=MESH)

    for load in loads:
        load.wait()

    base = (half + m) * tiles
    plate_row = plate[...]
    rank_row = rank[...]
    live = plate_row < plates
    slot_of = jnp.zeros_like(plate_row)
    for k in range(plates):
        slot_of = jnp.where(plate_row == k, owner_ref[k], slot_of)
    body_at = jnp.where(live, slot_of * pb + rank_row, plates * pb).astype(jnp.float32)
    live_f = live.astype(jnp.float32)
    packed = jnp.concatenate(
        [pos[...], force[...] * live_f, body_at, jnp.zeros_like(body_at)], axis=0
    )
    for t in range(tiles):
        ext[base + t] = packed[:, t * TILE : (t + 1) * TILE]

    @pl.when(jnp.logical_not(has_low))
    def _():
        ext[pl.ds(0, half * tiles)] = jnp.zeros((half * tiles, SUB, TILE), jnp.float32)

    @pl.when(jnp.logical_not(has_high))
    def _():
        ext[pl.ds((half + n_member) * tiles, half * tiles)] = jnp.zeros(
            (half * tiles, SUB, TILE), jnp.float32
        )

    for t in range(tiles):
        for c in range(3):
            row = packed[c : c + 1, t * TILE : (t + 1) * TILE]
            tgt[t * 3 + c] = jnp.broadcast_to(row, (TILE, TILE)).T

    def block(e):
        return ext.at[pl.ds(e * tiles, tiles)]

    def near_copy(step):
        return pltpu.make_async_remote_copy(
            src_ref=block(half + m),
            dst_ref=block(half + m),
            send_sem=send_sem.at[step],
            recv_sem=recv_sem.at[half + m],
            device_id=(r, lax.rem(m + step, n_member)),
            device_id_type=MESH,
        )

    def rim_copy(k, shift, e):
        return pltpu.make_async_remote_copy(
            src_ref=block(half + m),
            dst_ref=block(e),
            send_sem=send_sem.at[n_member + k],
            recv_sem=recv_sem.at[e],
            device_id=(r + shift, lax.rem(m + k, n_member)),
            device_id_type=MESH,
        )

    def arrival(e):
        return pltpu.make_async_remote_copy(
            src_ref=block(e),
            dst_ref=block(e),
            send_sem=send_sem.at[0],
            recv_sem=recv_sem.at[e],
            device_id=(r, lax.rem(m + 1, n_member)),
            device_id_type=MESH,
        )

    rim_sends = jnp.where(jnp.logical_or(to_high, to_low), n_member, 0)
    pl.semaphore_wait(barrier, n_member - 1 + rim_sends)

    @pl.when(to_high)
    def _():
        for k in range(n_member):
            rim_copy(k, 1, m - half).start()

    @pl.when(to_low)
    def _():
        for k in range(n_member):
            rim_copy(k, -1, half + n_member + m).start()

    for step in range(1, n_member):
        near_copy(step).start()

    def one_pair(t, s, tile_id, first):
        keep = jnp.where(s < count_ref[t], SCALE, 0.0)
        rows = ext[tile_id]

        def wide(c):
            return jnp.broadcast_to(rows[c : c + 1], (SUB, TILE))

        h = wide(2)
        src = (wide(0), wide(1), h, wide(3) * keep, wide(4) * keep, wide(5) * keep, h + h)
        for b in range(TILE // SUB):
            at = pl.ds(b * SUB, SUB)
            terms = pair_terms(tgt[t * 3, at], tgt[t * 3 + 1, at], tgt[t * 3 + 2, at], src)
            for c in range(3):
                if first:
                    acc[t * 3 + c, at] = terms[c]
                else:
                    acc[t * 3 + c, at] = acc[t * 3 + c, at] + terms[c]

    @pl.loop(0, tiles)
    def _(t):
        one_pair(t, 0, base + t, True)

    for step in range(1, n_member):
        arrival(half + lax.rem(m + step, n_member)).wait_recv()

    @pl.when(has_low)
    def _():
        for k in range(half):
            arrival(k).wait_recv()

    @pl.when(has_high)
    def _():
        for k in range(half):
            arrival(half + n_member + k).wait_recv()

    zeros = jnp.zeros((VROWS - 3, TILE), jnp.float32)

    def vel_copy(t, step, at):
        part = vel.at[:, pl.ds(pl.multiple_of(at * blobs + t * TILE, TILE), TILE)]
        return pltpu.make_async_remote_copy(
            src_ref=part,
            dst_ref=part,
            send_sem=vsend_sem.at[t, step],
            recv_sem=vrecv_sem.at[t, at],
            device_id=(r, lax.rem(m + step, n_member)),
            device_id_type=MESH,
        )

    @pl.loop(0, tiles)
    def _(t):
        for s in range(1, pairs):
            one_pair(t, s, list_ref[t, s], False)

    for t in range(tiles):
        rows = [jnp.sum(acc[t * 3 + c].T, axis=0, keepdims=True) for c in range(3)]
        at = pl.multiple_of(m * blobs + t * TILE, TILE)
        vel[:, pl.ds(at, TILE)] = jnp.concatenate(rows + [zeros], axis=0)
        vel_out[:, t * TILE : (t + 1) * TILE] = jnp.concatenate(rows, axis=0)
        for step in range(1, n_member):
            vel_copy(t, step, m).start()

    width = hot.shape[0] // own_plates
    place = lax.broadcasted_iota(jnp.int32, (hot.shape[0], TILE), 0)

    @pl.loop(0, n_member * tiles)
    def _(i):
        local = ext[half * tiles + i][6:7].astype(jnp.int32) - m * (own_plates * pb)
        row = jnp.full_like(local, -1)
        for k in range(own_plates):
            inside = jnp.logical_and(local >= k * pb, local < (k + 1) * pb)
            row = jnp.where(inside, local + k * (width - pb), row)
        at = pl.multiple_of(i * TILE, TILE)
        hot[:, pl.ds(at, TILE)] = jnp.where(place == row, 1.0, 0.0).astype(jnp.bfloat16)

    for step in range(1, n_member):
        for t in range(tiles):
            vel_copy(t, step, lax.rem(m + step, n_member)).wait_recv()

    placed = lax.dot_general(
        vel[...].astype(jnp.bfloat16),
        hot[...],
        (((1,), (1,)), ((), ())),
        preferred_element_type=jnp.float32,
    )
    order = 3 * pb
    total = 2 * width
    for k in range(own_plates):
        part = placed[:, k * width : (k + 1) * width]
        part = jnp.concatenate([part, jnp.zeros((VROWS, total - width), jnp.float32)], axis=1)
        body = part[0:1]
        for c in range(1, 3):
            body = body + pltpu.roll(part, c * pb, 1)[c : c + 1]
        body_out[k : k + 1] = body[:, :order]

    for step in range(1, n_member):
        near_copy(step).wait_send()
        for t in range(tiles):
            vel_copy(t, step, m).wait_send()

    @pl.when(to_high)
    def _():
        for k in range(n_member):
            rim_copy(k, 1, m - half).wait_send()

    @pl.when(to_low)
    def _():
        for k in range(n_member):
            rim_copy(k, -1, half + n_member + m).wait_send()


def finish(vel_ref, body_ref, vel_out, body_out):
    vel_out[...] = vel_ref[...]
    body_out[...] = body_ref[...]


def on_device(n_region, n_member, positions, forces, blob_platelet, blob_rank, owner, pair_list, pair_count, pre):
    blobs = positions.shape[1]
    tiles = blobs // TILE
    own_plates, order, _ = pre.shape
    pb = order // 3
    width = -(-pb // TILE) * TILE
    far = pl.BlockSpec(memory_space=pltpu.HBM)
    vector = pl.BlockSpec(memory_space=pltpu.VMEM)
    velocity, body_in = pl.pallas_call(
        functools.partial(kernel, n_region, n_member, pb, own_plates),
        out_shape=(
            pltpu.VMEM((3, blobs), jnp.float32),
            pltpu.VMEM((own_plates, order), jnp.float32),
        ),
        in_specs=[far] * 7,
        out_specs=(vector, vector),
        scratch_shapes=[
            pltpu.VMEM((3, blobs), jnp.float32),
            pltpu.VMEM((3, blobs), jnp.float32),
            pltpu.VMEM((1, blobs), jnp.int32),
            pltpu.VMEM((1, blobs), jnp.int32),
            pltpu.SMEM(owner.shape, jnp.int32),
            pltpu.SMEM(pair_list.shape, jnp.int32),
            pltpu.SMEM(pair_count.shape, jnp.int32),
            pltpu.VMEM((2 * n_member * tiles, SUB, TILE), jnp.float32),
            pltpu.VMEM((3 * tiles, TILE, TILE), jnp.float32),
            pltpu.VMEM((3 * tiles, TILE, TILE), jnp.float32),
            pltpu.VMEM((VROWS, n_member * blobs), jnp.float32),
            pltpu.VMEM((own_plates * width, n_member * blobs), jnp.bfloat16),
            pltpu.SemaphoreType.DMA((7,)),
            pltpu.SemaphoreType.DMA((2 * n_member,)),
            pltpu.SemaphoreType.DMA((2 * n_member,)),
            pltpu.SemaphoreType.DMA((tiles, n_member)),
            pltpu.SemaphoreType.DMA((tiles, n_member)),
        ],
        compiler_params=pltpu.CompilerParams(collective_id=0, has_side_effects=True),
    )(
        positions,
        forces,
        blob_platelet,
        blob_rank,
        owner,
        pair_list,
        pair_count,
    )
    body_velocity = jnp.einsum(
        "pab,pb->pa", pre, body_in.astype(jnp.bfloat16), preferred_element_type=jnp.float32
    )
    return pl.pallas_call(
        finish,
        out_shape=(
            jax.ShapeDtypeStruct(velocity.shape, jnp.float32),
            jax.ShapeDtypeStruct(body_velocity.shape, jnp.float32),
        ),
        in_specs=[vector, vector],
        out_specs=(vector, vector),
        compiler_params=pltpu.CompilerParams(vmem_limit_bytes=1024 * 1024),
    )(velocity, body_velocity)


def solution(mesh):
    placed = (
        P(None, ("region", "member")),
        P(None, ("region", "member")),
        P(("region", "member")),
        P(("region", "member")),
        P("region"),
        P(("region", "member"), None),
        P(("region", "member")),
        P(("region", "member"), None, None),
    )
    return jax.shard_map(
        functools.partial(on_device, mesh.shape["region"], mesh.shape["member"]),
        mesh=mesh,
        in_specs=placed,
        out_specs=(P(None, ("region", "member")), P(("region", "member"), None)),
        check_vma=False,
    )
```
